32 devices in a mesh: lon: 8 (over z, y), lat: 4 (over x, core).
Axes of the slice: x: 2, y: 2, z: 4, core: 2. Of those that a mesh axis runs over, the one named last changes fastest.
Arguments:
- fields_in: bfloat16 [2, 48, 192, 512], P(None, 'lat', 'lon'), may hold values from -6 to 6
- level_map: int32 [2, 48, 192], P(None, 'lat', 'lon'), may hold values from 0 to 12
- land_sea: int32 [48, 192], P('lat', 'lon'), may hold values 0 or 1
- level_table: bfloat16 [13, 512], replicated, may hold values from -4 to 4
- surface_table: bfloat16 [2, 512], replicated, may hold values from -4 to 4
- norm_gain: bfloat16 [512], replicated, may hold values from 0.25 to 1.75
- w_qkv: bfloat16 [512, 1536], replicated, may hold values from -1 to 1
- w_proj: bfloat16 [512, 512], replicated, may hold values from -0.25 to 0.25
- merge_gain: bfloat16 [2048], replicated, may hold values from 0.25 to 1.75
- w_merge: bfloat16 [2048, 1024], replicated, may hold values from -0.125 to 0.125
- coarse_gain: bfloat16 [1024], replicated, may hold values from 0.25 to 1.75
- w_in: bfloat16 [1024, 4096], P(None, 'lat'), may hold values from -0.1875 to 0.1875
- w_out: bfloat16 [4096, 1024], P('lat'), may hold values from -0.09375 to 0.09375
- w_expand: bfloat16 [1024, 2048], replicated, may hold values from -0.1875 to 0.1875
- cotangent: bfloat16 [2, 48, 192, 512], P(None, 'lat', 'lon'), may hold values from -6 to 6
Outputs:
- fields_out: bfloat16 [2, 48, 192, 512], P(None, 'lat', 'lon')
- grad_in: float32 [1024, 4096], P('lon', 'lat')
- grad_out: float32 [4096, 1024], P('lat', 'lon')
The draws below stay inside these ranges and needn't reach their ends.
All inputs are finite; a program needn't handle non-finite values. No bound on the sum of `land_sea` on one device may be relied on, other than what follows from the above.
Results may differ from the reference program's by a relative error of at most 0.025.
Values may be sent and summed in bfloat16 or wider, within the bound.
A program may use at most 128 MiB of HBM per device.

```python
import math
import jax
import jax.numpy as jnp
from jax import lax

C1 = 512
C2 = 1024
FF2 = 4096
HEADS = 8
NLEV = 13
LEVELS = 2
WIN_LAT = 12
WIN_LON = 6
SHIFT_LAT = 6
SHIFT_LON = 3
LAT = 48
LON = 192


def draw_w_qkv(key, part):
    first = jax.random.fold_in(key, 0)
    base = jax.random.normal(first, (C1, 3 * C1), jnp.float32) * C1 ** (-0.5)
    return jnp.clip(base, -1.0, 1.0).astype(jnp.bfloat16)


def with_ends(values, key, least, largest):
    longest = values.shape.index(max(values.shape))
    spots = []
    for shift in (0, 1):
        where = [jax.random.randint(jax.random.fold_in(key, axis), (), 0, length) for axis, length in enumerate(values.shape)]
        where[longest] = (where[longest] + shift) % values.shape[longest]
        spots.append(tuple(where))
    return values.at[spots[0]].set(least).at[spots[1]].set(largest)


def shard_levels(rng, extent, cuts, smallest, top_value):
    level = 1.0
    for axis_at, parts in cuts:
        heights = jax.random.uniform(jax.random.fold_in(jax.random.fold_in(rng, 6), axis_at), (parts,), jnp.float32, smallest / len(cuts), top_value / len(cuts))
        level = level * jnp.repeat(jnp.exp(heights), extent[axis_at] // parts).reshape((-1,) + (1,) * (len(extent) - 1 - axis_at))
    return level


def scatter_about(own_key, extent, scale, most, shards=(), kind=jnp.bfloat16):
    result = scale * jax.random.normal(own_key, extent, jnp.float32)
    if shards:
        result = result * shard_levels(own_key, extent, shards, -0.22, 0.18)
    return jnp.clip(result, -most, most).astype(kind)


def setup_inputs(seed: int = 0) -> dict:
    key_list = jax.random.split(jax.random.key(seed), 16)
    fields_in = scatter_about(key_list[0], (LEVELS, LAT, LON, C1), 1.0, 6.0, ((1, 4), (2, 8)))
    level_map = with_ends(jax.random.randint(key_list[1], (LEVELS, LAT, LON), 0, NLEV), jax.random.fold_in(key_list[1], 1), 0, NLEV - 1).astype(jnp.int32)
    land_sea = with_ends((jax.random.randint(key_list[2], (LAT, LON), 0, 3) < 1).astype(jnp.int32), jax.random.fold_in(key_list[2], 1), 0, 1)
    level_table = scatter_about(key_list[3], (NLEV, C1), 0.7, 4.0)
    surface_table = scatter_about(key_list[4], (2, C1), 0.7, 4.0)
    norm_gain = jnp.clip(1.0 + 0.15 * jax.random.normal(key_list[5], (C1,), jnp.float32), 0.25, 1.75).astype(jnp.bfloat16)
    w_qkv = draw_w_qkv(jax.random.fold_in(key_list[15], 71), 0)
    w_proj = scatter_about(key_list[7], (C1, C1), C1 ** -0.5, 0.25)
    merge_gain = jnp.clip(1.0 + 0.15 * jax.random.normal(key_list[8], (4 * C1,), jnp.float32), 0.25, 1.75).astype(jnp.bfloat16)
    w_merge = scatter_about(key_list[9], (4 * C1, C2), (4 * C1) ** -0.5, 0.125)
    coarse_gain = jnp.clip(1.0 + 0.15 * jax.random.normal(key_list[10], (C2,), jnp.float32), 0.25, 1.75).astype(jnp.bfloat16)
    w_in = scatter_about(key_list[11], (C2, FF2), C2 ** -0.5, 0.1875, ((1, 4),))
    w_out = scatter_about(key_list[12], (FF2, C2), FF2 ** -0.5, 0.09375, ((0, 4),))
    w_expand = scatter_about(key_list[13], (C2, 4 * C1), C2 ** -0.5, 0.1875)
    cotangent = scatter_about(key_list[14], (LEVELS, LAT, LON, C1), 1.0, 6.0, ((1, 4), (2, 8)))
    return {"fields_in": fields_in, "level_map": level_map, "land_sea": land_sea, "level_table": level_table, "surface_table": surface_table, "norm_gain": norm_gain, "w_qkv": w_qkv, "w_proj": w_proj, "merge_gain": merge_gain, "w_merge": w_merge, "coarse_gain": coarse_gain, "w_in": w_in, "w_out": w_out, "w_expand": w_expand, "cotangent": cotangent}


EPSILON = 1e-05

def layer_norm(values, gain):
    center = values - lax.optimization_barrier(jnp.mean(values, axis=-1, keepdims=True))
    spread = lax.optimization_barrier(jnp.mean(center * center, axis=-1, keepdims=True))
    return center * lax.rsqrt(spread + EPSILON) * gain.astype(jnp.float32)

def activate(values):
    return jax.nn.gelu(values, approximate=True)

def window_attention(packed, lat_index, lat_total):
    levels, rows, cols, triple = packed.shape
    width = triple // 3
    head_size = width // HEADS
    count_rows = rows // WIN_LAT
    count_cols = cols // WIN_LON
    window = levels * WIN_LAT * WIN_LON
    blocks = packed.reshape(levels, count_rows, WIN_LAT, count_cols, WIN_LON, triple)
    blocks = blocks.transpose(1, 3, 0, 2, 4, 5).reshape(count_rows * count_cols, window, triple)
    blocks = blocks.astype(jnp.float32)
    queries = blocks[:, :, :width].reshape(-1, window, HEADS, head_size)
    keys = blocks[:, :, width:2 * width].reshape(-1, window, HEADS, head_size)
    values = blocks[:, :, 2 * width:].reshape(-1, window, HEADS, head_size)
    scores = jnp.einsum('wqhd,wkhd->whqk', queries, keys) * (1.0 / math.sqrt(head_size))
    token_row = jnp.arange(window, dtype=jnp.int32) // WIN_LON % WIN_LAT
    block_row = jnp.arange(count_rows * count_cols, dtype=jnp.int32) // count_cols
    global_row = lat_index * rows + block_row[:, None] * WIN_LAT + token_row[None, :]
    region = (global_row >= lat_total - WIN_LAT).astype(jnp.int32) + (global_row >= lat_total - SHIFT_LAT).astype(jnp.int32)
    same = region[:, :, None] == region[:, None, :]
    scores = jnp.where(same[:, None], scores, -1e+30)
    top = lax.optimization_barrier(jnp.max(scores, axis=-1, keepdims=True))
    expos = jnp.exp(scores - top)
    probs = (expos / lax.optimization_barrier(jnp.sum(expos, axis=-1, keepdims=True))).astype(jnp.bfloat16)
    mixed = jnp.einsum('whqk,wkhd->wqhd', probs.astype(jnp.float32), values).astype(jnp.bfloat16)
    mixed = mixed.reshape(count_rows, count_cols, levels, WIN_LAT, WIN_LON, width)
    return mixed.transpose(2, 0, 3, 1, 4, 5).reshape(levels, rows, cols, width)

def merge_tokens(grid):
    levels, rows, cols, width = grid.shape
    blocks = grid.reshape(levels, rows // 2, 2, cols // 2, 2, width).transpose(0, 1, 3, 4, 2, 5)
    return blocks.reshape(-1, 4 * width)

def split_tokens(tokens, levels, rows, cols):
    width = tokens.shape[-1] // 4
    blocks = tokens.reshape(levels, rows // 2, cols // 2, 2, 2, width).transpose(0, 1, 4, 2, 3, 5)
    return blocks.reshape(levels, rows, cols, width)

def reference(fields_in, level_map, land_sea, level_table, surface_table, norm_gain, w_qkv, w_proj, merge_gain, w_merge, coarse_gain, w_in, w_out, w_expand, cotangent):
    width = fields_in.shape[-1]
    level_bias = level_table.astype(jnp.float32)[level_map]
    surface_bias = jnp.where(land_sea[..., None] == 1, surface_table[1].astype(jnp.float32), surface_table[0].astype(jnp.float32))
    fields = fields_in.astype(jnp.float32) + level_bias + surface_bias[None]
    normed = layer_norm(fields, norm_gain).astype(jnp.bfloat16)
    packed = jnp.dot(normed.reshape(-1, width), w_qkv, preferred_element_type=jnp.float32).astype(jnp.bfloat16)
    packed = packed.reshape(LEVELS, LAT, LON, 3 * width)
    rolled = jnp.roll(packed, (-SHIFT_LAT, -SHIFT_LON), axis=(1, 2))
    stacked = rolled.reshape(LEVELS, LAT // WIN_LAT, WIN_LAT, LON, 3 * width).transpose(1, 0, 2, 3, 4)
    index_rows = jnp.arange(LAT // WIN_LAT, dtype=jnp.int32)
    attended = lax.map(lambda pair: window_attention(pair[0], pair[1], LAT), (stacked, index_rows))
    attended = attended.transpose(1, 0, 2, 3, 4).reshape(LEVELS, LAT, LON, width)
    attended = jnp.roll(attended, (SHIFT_LAT, SHIFT_LON), axis=(1, 2))
    projected = jnp.dot(attended.reshape(-1, width), w_proj, preferred_element_type=jnp.float32)
    skip = (fields + projected.reshape(fields.shape)).astype(jnp.bfloat16)
    merged_normed = layer_norm(merge_tokens(skip).astype(jnp.float32), merge_gain).astype(jnp.bfloat16)
    coarse = jnp.dot(merged_normed, w_merge, preferred_element_type=jnp.float32).astype(jnp.bfloat16)
    coarse_normed = layer_norm(coarse.astype(jnp.float32), coarse_gain).astype(jnp.bfloat16)
    act = jnp.dot(coarse_normed, w_in, preferred_element_type=jnp.float32)
    hidden = activate(act).astype(jnp.bfloat16)
    coarse_out = (coarse.astype(jnp.float32) + jnp.dot(hidden, w_out, preferred_element_type=jnp.float32)).astype(jnp.bfloat16)
    expanded = jnp.dot(coarse_out, w_expand, preferred_element_type=jnp.float32)
    fields_out = (skip.astype(jnp.float32) + split_tokens(expanded, LEVELS, LAT, LON)).astype(jnp.bfloat16)
    cot_tokens = merge_tokens(cotangent)
    d_coarse = jnp.dot(cot_tokens, w_expand.T, preferred_element_type=jnp.float32).astype(jnp.bfloat16)
    d_hidden = jnp.dot(d_coarse, w_out.T, preferred_element_type=jnp.float32)
    unused, pullback = jax.vjp(activate, act)
    d_act = pullback(d_hidden)[0].astype(jnp.bfloat16)
    grad_out = jnp.dot(hidden.T, d_coarse, preferred_element_type=jnp.float32)
    grad_in = jnp.dot(coarse_normed.T, d_act, preferred_element_type=jnp.float32)
    return (fields_out, grad_in, grad_out)
```

```python
import math

import jax
import jax.numpy as jnp
from jax import lax
from jax.sharding import PartitionSpec as P


HEADS = 8
WIN_LAT = 12
WIN_LON = 6
SHIFT_LAT = 6
SHIFT_LON = 3


EPSILON = 1e-05


def passed_along(value, axis, steps):
    count = lax.axis_size(axis)
    pairs = [(source, (source + steps) % count) for source in range(count)]
    return lax.ppermute(value, axis, pairs)


def layer_norm(values, gain):
    center = values - jnp.mean(values, axis=-1, keepdims=True)
    spread = jnp.mean(center * center, axis=-1, keepdims=True)
    return center * lax.rsqrt(spread + EPSILON) * gain.astype(jnp.float32)


def activate(values):
    return jax.nn.gelu(values, approximate=True)


def corner_pairs(steps):
    lats, lons = lax.axis_size("lat"), lax.axis_size("lon")
    return [
        (b * lats + a, (b + steps) % lons * lats + (a + steps) % lats)
        for a in range(lats)
        for b in range(lons)
    ]


def rolled_tile(grid, offset):
    if offset < 0:
        near_rows, near_cols = grid[:, :SHIFT_LAT], grid[:, :, :SHIFT_LON]
        rest_rows, rest_cols = grid[:, SHIFT_LAT:], grid[:, :, SHIFT_LON:]
        own = rest_rows[:, :, SHIFT_LON:]
    else:
        near_rows = grid[:, grid.shape[1] - SHIFT_LAT :]
        near_cols = grid[:, :, grid.shape[2] - SHIFT_LON :]
        rest_rows = grid[:, : grid.shape[1] - SHIFT_LAT]
        rest_cols = grid[:, :, : grid.shape[2] - SHIFT_LON]
        own = rest_rows[:, :, : grid.shape[2] - SHIFT_LON]
    if offset < 0:
        send_row, send_col = near_rows[:, :, SHIFT_LON:], near_cols[:, SHIFT_LAT:]
        send_corner = near_rows[:, :, :SHIFT_LON]
    else:
        send_row = near_rows[:, :, : grid.shape[2] - SHIFT_LON]
        send_col = near_cols[:, : grid.shape[1] - SHIFT_LAT]
        send_corner = near_rows[:, :, grid.shape[2] - SHIFT_LON :]
    got_row = passed_along(send_row, "lat", offset)
    got_corner = lax.ppermute(send_corner, ("lon", "lat"), corner_pairs(offset))
    got_col = passed_along(send_col, "lon", offset)
    if offset < 0:
        top = jnp.concatenate([own, got_col], axis=2)
        bottom = jnp.concatenate([got_row, got_corner], axis=2)
    else:
        bottom = jnp.concatenate([got_col, own], axis=2)
        top = jnp.concatenate([got_corner, got_row], axis=2)
    return jnp.concatenate([top, bottom], axis=1)


def swapped(value, axis, bit):
    return lax.ppermute(value, axis, [(place, place ^ bit) for place in range(lax.axis_size(axis))])


def gathered_pieces(block, axis):
    pieces = [block]
    bit = lax.axis_size(axis) // 2
    while bit:
        pieces = pieces + [swapped(piece, axis, bit) for piece in pieces]
        bit //= 2
    return jnp.concatenate(pieces, axis=0)


def scattered_pieces(total, axis):
    bit = 1
    while bit < lax.axis_size(axis):
        half = total.shape[0] // 2
        got = swapped(total[half:].astype(jnp.bfloat16), axis, bit)
        total = total[:half] + got.astype(jnp.float32)
        bit *= 2
    return total


def scattered_blocks(total, axis):
    count = lax.axis_size(axis)
    place = lax.axis_index(axis)
    total = total.reshape((count, total.shape[0] // count) + total.shape[1:])
    bit = 1
    while bit < count:
        pairs = total.reshape((total.shape[0] // 2, 2) + total.shape[1:])
        mine = place // bit % 2
        send = lax.dynamic_index_in_dim(pairs, 1 - mine, 1, keepdims=False)
        keep = lax.dynamic_index_in_dim(pairs, mine, 1, keepdims=False)
        got = swapped(send.astype(jnp.bfloat16), axis, bit)
        total = keep.astype(jnp.float32) + got.astype(jnp.float32)
        bit *= 2
        if bit < count:
            total = total.astype(jnp.bfloat16)
    return total[0]


def window_attention(packed, lat_index, lat_total):
    levels, rows, cols, triple = packed.shape
    width = triple // 3
    head_size = width // HEADS
    count_rows = rows // WIN_LAT
    count_cols = cols // WIN_LON
    window = levels * WIN_LAT * WIN_LON
    blocks = packed.reshape(levels, count_rows, WIN_LAT, count_cols, WIN_LON, triple)
    blocks = blocks.transpose(1, 3, 0, 2, 4, 5).reshape(count_rows * count_cols, window, triple)
    queries = blocks[:, :, :width].reshape(-1, window, HEADS, head_size)
    keys = blocks[:, :, width : 2 * width].reshape(-1, window, HEADS, head_size)
    values = blocks[:, :, 2 * width :].reshape(-1, window, HEADS, head_size)
    scores = jnp.einsum("wqhd,wkhd->whqk", queries, keys, preferred_element_type=jnp.float32) * (
        1.0 / math.sqrt(head_size)
    )
    token_row = jnp.arange(window, dtype=jnp.int32) // WIN_LON % WIN_LAT
    block_row = jnp.arange(count_rows * count_cols, dtype=jnp.int32) // count_cols
    global_row = lat_index * rows + block_row[:, None] * WIN_LAT + token_row[None, :]
    region = (global_row >= lat_total - WIN_LAT).astype(jnp.int32) + (
        global_row >= lat_total - SHIFT_LAT
    ).astype(jnp.int32)
    same = region[:, :, None] == region[:, None, :]
    scores = jnp.where(same[:, None], scores, -1e30)
    top = jnp.max(scores, axis=-1, keepdims=True)
    expos = jnp.exp(scores - top)
    probs = (expos / jnp.sum(expos, axis=-1, keepdims=True)).astype(jnp.bfloat16)
    mixed = jnp.einsum("whqk,wkhd->wqhd", probs, values, preferred_element_type=jnp.float32).astype(
        jnp.bfloat16
    )
    mixed = mixed.reshape(count_rows, count_cols, levels, WIN_LAT, WIN_LON, width)
    return mixed.transpose(2, 0, 3, 1, 4, 5).reshape(levels, rows, cols, width)


def merge_tokens(grid):
    levels, rows, cols, width = grid.shape
    blocks = grid.reshape(levels, rows // 2, 2, cols // 2, 2, width).transpose(0, 1, 3, 4, 2, 5)
    return blocks.reshape(-1, 4 * width)


def split_tokens(tokens, levels, rows, cols):
    width = tokens.shape[-1] // 4
    blocks = tokens.reshape(levels, rows // 2, cols // 2, 2, 2, width).transpose(0, 1, 4, 2, 3, 5)
    return blocks.reshape(levels, rows, cols, width)


def on_device(
    fields_in,
    level_map,
    land_sea,
    level_table,
    surface_table,
    norm_gain,
    w_qkv,
    w_proj,
    merge_gain,
    w_merge,
    coarse_gain,
    w_in,
    w_out,
    w_expand,
    cotangent,
):
    levels, rows, cols, width = fields_in.shape
    cot_tokens = merge_tokens(cotangent)
    d_coarse = jnp.einsum(
        "tk,ck->tc", cot_tokens, w_expand, preferred_element_type=jnp.float32
    ).astype(jnp.bfloat16)
    d_gathered = gathered_pieces(d_coarse, "lat")
    table_rows = level_table.shape[0]
    one_hot = (level_map[..., None] == jnp.arange(table_rows, dtype=jnp.int32)).astype(jnp.bfloat16)
    level_bias = jnp.dot(
        one_hot.reshape(-1, table_rows), level_table, preferred_element_type=jnp.float32
    )
    level_bias = level_bias.reshape(levels, rows, cols, width)
    surface_bias = jnp.where(
        land_sea[..., None] == 1,
        surface_table[1].astype(jnp.float32),
        surface_table[0].astype(jnp.float32),
    )
    fields = fields_in.astype(jnp.float32) + level_bias + surface_bias[None]
    normed = layer_norm(fields, norm_gain).astype(jnp.bfloat16)
    moved = rolled_tile(normed, -1)
    shifted = jnp.dot(moved.reshape(-1, width), w_qkv, preferred_element_type=jnp.float32).astype(
        jnp.bfloat16
    )
    shifted = shifted.reshape(levels, rows, cols, 3 * width)
    lat_total = rows * lax.axis_size("lat")
    attended = window_attention(shifted, lax.axis_index("lat"), lat_total)
    attended = rolled_tile(attended, 1)
    projected = jnp.dot(attended.reshape(-1, width), w_proj, preferred_element_type=jnp.float32)
    skip = (fields + projected.reshape(fields.shape)).astype(jnp.bfloat16)
    merged_normed = layer_norm(merge_tokens(skip).astype(jnp.float32), merge_gain).astype(
        jnp.bfloat16
    )
    coarse = jnp.dot(merged_normed, w_merge, preferred_element_type=jnp.float32).astype(
        jnp.bfloat16
    )
    coarse_normed = layer_norm(coarse.astype(jnp.float32), coarse_gain).astype(jnp.bfloat16)
    gathered = gathered_pieces(coarse_normed, "lat")
    act = jnp.dot(gathered, w_in, preferred_element_type=jnp.float32)
    hidden = activate(act).astype(jnp.bfloat16)
    d_hidden = jnp.einsum("tc,fc->tf", d_gathered, w_out, preferred_element_type=jnp.float32)
    unused, pullback = jax.vjp(activate, act)
    d_act = pullback(d_hidden)[0].astype(jnp.bfloat16)

    def gradient(left, right):
        half = right.shape[1] // 2
        parts = [
            scattered_blocks(
                jnp.einsum(
                    "tc,tf->cf", left, right[:, start : start + half],
                    preferred_element_type=jnp.float32,
                ).astype(jnp.bfloat16),
                "lon",
            )
            for start in (0, half)
        ]
        return jnp.concatenate(parts, axis=1)

    grad_out = gradient(d_gathered, hidden).T
    grad_in = gradient(gathered, d_act)
    mixed = scattered_pieces(jnp.dot(hidden, w_out, preferred_element_type=jnp.float32), "lat")
    coarse_out = (coarse.astype(jnp.float32) + mixed).astype(jnp.bfloat16)
    expanded = jnp.dot(coarse_out, w_expand, preferred_element_type=jnp.float32)
    fields_out = (skip.astype(jnp.float32) + split_tokens(expanded, levels, rows, cols)).astype(
        jnp.bfloat16
    )
    return (fields_out, grad_in, grad_out)


def solution(mesh):
    placed = (
        P(None, "lat", "lon", None),
        P(None, "lat", "lon"),
        P("lat", "lon"),
        P(),
        P(),
        P(),
        P(),
        P(),
        P(),
        P(),
        P(),
        P(None, "lat"),
        P("lat", None),
        P(),
        P(None, "lat", "lon", None),
    )
    return jax.shard_map(
        on_device,
        mesh=mesh,
        in_specs=placed,
        out_specs=(P(None, "lat", "lon", None), P("lon", "lat"), P("lat", "lon")),
        check_vma=False,
    )
```

```python
import functools
import math

import jax
import jax.numpy as jnp
import numpy as np
from jax import lax
from jax.experimental import pallas as pl
from jax.experimental.pallas import tpu as pltpu
from jax.sharding import PartitionSpec as P


HEADS = 8
WIN_LAT = 12
WIN_LON = 6
SHIFT_LAT = 6
SHIFT_LON = 3


EPSILON = 1e-05


def passed_along(value, axis, steps):
    count = lax.axis_size(axis)
    pairs = [(source, (source + steps) % count) for source in range(count)]
    return lax.ppermute(value, axis, pairs)


def layer_norm(values, gain):
    center = values - jnp.mean(values, axis=-1, keepdims=True)
    spread = jnp.mean(center * center, axis=-1, keepdims=True)
    return center * lax.rsqrt(spread + EPSILON) * gain.astype(jnp.float32)


def activate(values):
    return jax.nn.gelu(values, approximate=True)


def corner_pairs(steps):
    lats, lons = lax.axis_size("lat"), lax.axis_size("lon")
    return [
        (b * lats + a, (b + steps) % lons * lats + (a + steps) % lats)
        for a in range(lats)
        for b in range(lons)
    ]


def swapped(value, axis, bit):
    return lax.ppermute(value, axis, [(place, place ^ bit) for place in range(lax.axis_size(axis))])


def gathered_pieces(block, axis):
    pieces = [block]
    bit = lax.axis_size(axis) // 2
    while bit:
        pieces = pieces + [swapped(piece, axis, bit) for piece in pieces]
        bit //= 2
    return jnp.concatenate(pieces, axis=0)


def scattered_pieces(total, axis):
    bit = 1
    while bit < lax.axis_size(axis):
        half = total.shape[0] // 2
        got = swapped(total[half:].astype(jnp.bfloat16), axis, bit)
        total = total[:half] + got.astype(jnp.float32)
        bit *= 2
    return total


def scattered_blocks(total, axis):
    count = lax.axis_size(axis)
    place = lax.axis_index(axis)
    total = total.reshape((count, total.shape[0] // count) + total.shape[1:])
    bit = 1
    while bit < count:
        pairs = total.reshape((total.shape[0] // 2, 2) + total.shape[1:])
        mine = place // bit % 2
        send = lax.dynamic_index_in_dim(pairs, 1 - mine, 1, keepdims=False)
        keep = lax.dynamic_index_in_dim(pairs, mine, 1, keepdims=False)
        got = swapped(send.astype(jnp.bfloat16), axis, bit)
        total = keep.astype(jnp.float32) + got.astype(jnp.float32)
        bit *= 2
        if bit < count:
            total = total.astype(jnp.bfloat16)
    return total[0]


class TokenOrder:
    def __init__(self, levels, rows, cols):
        self.levels, self.rows, self.cols = levels, rows, cols
        grid = np.arange(levels * rows * cols).reshape(levels, rows, cols)
        blocks = grid.reshape(levels, rows // 2, 2, cols // 2, 2)
        self.merging = blocks.transpose(4, 2, 0, 1, 3).reshape(-1)
        self.unmerging = np.argsort(self.merging)
        place = self.unmerging.reshape(levels, rows, cols)
        windows = grid.reshape(
            levels, rows // WIN_LAT, WIN_LAT, cols // WIN_LON, WIN_LON
        ).transpose(1, 3, 0, 2, 4)
        self.windows = windows.reshape(-1)
        held = np.argsort(self.windows).reshape(levels, rows, cols)
        near, far = slice(None, SHIFT_LAT), slice(SHIFT_LAT, None)
        left, right = slice(None, SHIFT_LON), slice(SHIFT_LON, None)
        self.out_picks, base = self.picks(place, near, far, left, right)
        rolled = np.block([[[place[:, far, right], base[1]], [base[0], base[2]]]])
        self.to_windows = rolled.reshape(-1)[self.windows]
        top, last = slice(None, rows - SHIFT_LAT), slice(rows - SHIFT_LAT, None)
        west, east = slice(None, cols - SHIFT_LON), slice(cols - SHIFT_LON, None)
        self.back_picks, base = self.picks(held, last, top, east, west)
        unrolled = np.block([[[base[2], base[0]], [base[1], held[:, top, west]]]])
        self.to_merging = unrolled.reshape(-1)[self.merging]

    def picks(self, place, edge_rows, inner_rows, edge_cols, inner_cols):
        parts = (
            place[:, edge_rows, inner_cols],
            place[:, inner_rows, edge_cols],
            place[:, edge_rows, edge_cols],
        )
        start, chosen, base = place.size, [], []
        for part in parts:
            padded = -(-part.size // 16) * 16
            chosen.append(np.concatenate([part.reshape(-1), np.full(padded - part.size, -1)]))
            base.append(start + np.arange(part.size).reshape(part.shape))
            start += padded
        return chosen, base


def picked(places, tokens):
    where = jnp.asarray(places, dtype=jnp.int32)
    chosen = where[:, None] == jnp.arange(tokens.shape[0], dtype=jnp.int32)[None, :]
    return jnp.dot(chosen.astype(jnp.bfloat16), tokens, preferred_element_type=jnp.float32).astype(
        jnp.bfloat16
    )


def with_halo(tokens, picks, offset):
    sizes = [len(pick) for pick in picks]
    edges = picked(np.concatenate(picks), tokens)
    row, col = edges[: sizes[0]], edges[sizes[0] : sizes[0] + sizes[1]]
    corner = edges[sizes[0] + sizes[1] :]
    got_row = passed_along(row, "lat", offset)
    got_col = passed_along(col, "lon", offset)
    got_corner = lax.ppermute(corner, ("lon", "lat"), corner_pairs(offset))
    return jnp.concatenate([tokens, got_row, got_col, got_corner], axis=0)


def attention_kernel(width, tokens_ref, weight_ref, mask_ref, out_ref):
    head_size = width // HEADS
    lanes = 2 * head_size
    packed = jnp.dot(tokens_ref[...], weight_ref[...], preferred_element_type=jnp.float32)
    queries = (packed[:, :width] * (1.0 / math.sqrt(head_size))).astype(jnp.bfloat16)
    keys = packed[:, width : 2 * width].astype(jnp.bfloat16)
    values = packed[:, 2 * width :].astype(jnp.bfloat16)
    mask = mask_ref[...]
    first = lax.broadcasted_iota(jnp.int32, (tokens_ref.shape[0], lanes), 1) < head_size
    for pair in range(HEADS // 2):
        span = slice(pair * lanes, (pair + 1) * lanes)
        both, key, value = queries[:, span], keys[:, span], values[:, span]
        results = []
        for query in (jnp.where(first, both, 0), jnp.where(first, 0, both)):
            scores = lax.dot_general(
                query.astype(jnp.bfloat16), key, (((1,), (1,)), ((), ())),
                preferred_element_type=jnp.float32,
            )
            scores = scores + mask
            expos = jnp.exp(scores - jnp.max(scores, axis=-1, keepdims=True))
            total = jnp.sum(expos, axis=-1, keepdims=True)
            mixed = jnp.dot(expos.astype(jnp.bfloat16), value, preferred_element_type=jnp.float32)
            results.append(mixed * (1.0 / total))
        out_ref[:, span] = jnp.where(first, results[0], results[1]).astype(jnp.bfloat16)


def window_attention(tokens, w_qkv, levels, rows, cols, lat_index, lat_total):
    width = tokens.shape[1]
    window = levels * WIN_LAT * WIN_LON
    count_rows, count_cols = rows // WIN_LAT, cols // WIN_LON
    token_row = jnp.arange(window, dtype=jnp.int32) // WIN_LON % WIN_LAT
    block_row = jnp.arange(count_rows, dtype=jnp.int32)
    global_row = lat_index * rows + block_row[:, None] * WIN_LAT + token_row[None, :]
    region = (global_row >= lat_total - WIN_LAT).astype(jnp.int32) + (
        global_row >= lat_total - SHIFT_LAT
    ).astype(jnp.int32)
    mask = jnp.where(region[:, :, None] == region[:, None, :], 0.0, -1e30).astype(jnp.float32)
    return pl.pallas_call(
        functools.partial(attention_kernel, width),
        out_shape=jax.ShapeDtypeStruct(tokens.shape, jnp.bfloat16),
        grid=(count_rows * count_cols,),
        in_specs=[
            pl.BlockSpec((window, width), lambda step: (step, 0)),
            pl.BlockSpec(w_qkv.shape, lambda step: (0, 0)),
            pl.BlockSpec((None, window, window), lambda step: (step // count_cols, 0, 0)),
        ],
        out_specs=pl.BlockSpec((window, width), lambda step: (step, 0)),
        cost_estimate=pl.CostEstimate(
            flops=2 * tokens.shape[0] * width * (3 * width + 2 * window),
            bytes_accessed=4 * tokens.size + 2 * w_qkv.size,
            transcendentals=tokens.shape[0] * window * HEADS,
        ),
    )(tokens, w_qkv, mask)


def side_by_side(tokens):
    count = tokens.shape[0] // 4
    return jnp.concatenate([tokens[part * count : (part + 1) * count] for part in range(4)], axis=1)


def on_device(
    fields_in,
    level_map,
    land_sea,
    level_table,
    surface_table,
    norm_gain,
    w_qkv,
    w_proj,
    merge_gain,
    w_merge,
    coarse_gain,
    w_in,
    w_out,
    w_expand,
    cotangent,
):
    levels, rows, cols, width = fields_in.shape
    count = levels * rows * cols
    order = TokenOrder(levels, rows, cols)
    table_rows = level_table.shape[0]
    level_hot = level_map[..., None] == jnp.arange(table_rows, dtype=jnp.int32)
    sea_hot = (land_sea[..., None] == 1) == (jnp.arange(2, dtype=jnp.int32) == 1)
    sea_hot = jnp.broadcast_to(sea_hot[None], (levels, rows, cols, 2))
    hot = jnp.concatenate([level_hot, sea_hot], axis=-1).astype(jnp.bfloat16)
    hot = picked(order.merging, hot.reshape(count, table_rows + 2))
    tables = jnp.concatenate([level_table, surface_table], axis=0)
    bias = jnp.dot(hot, tables, preferred_element_type=jnp.float32)
    fields = picked(order.merging, fields_in.reshape(count, width)).astype(jnp.float32) + bias
    normed = layer_norm(fields, norm_gain).astype(jnp.bfloat16)
    halo = with_halo(normed, order.out_picks, -1)
    cot_tokens = side_by_side(picked(order.merging, cotangent.reshape(count, width)))
    d_coarse = jnp.einsum(
        "tk,ck->tc", cot_tokens, w_expand, preferred_element_type=jnp.float32
    ).astype(jnp.bfloat16)
    halo, d_coarse = lax.optimization_barrier((halo, d_coarse))
    d_gathered = gathered_pieces(d_coarse, "lat")
    windows = picked(order.to_windows, halo)
    lat_total = rows * lax.axis_size("lat")
    attended = window_attention(
        windows, w_qkv, levels, rows, cols, lax.axis_index("lat"), lat_total
    )
    attended = picked(order.to_merging, with_halo(attended, order.back_picks, 1))
    projected = jnp.dot(attended, w_proj, preferred_element_type=jnp.float32)
    skip = (fields + projected).astype(jnp.bfloat16)
    merged_normed = layer_norm(side_by_side(skip).astype(jnp.float32), merge_gain).astype(
        jnp.bfloat16
    )
    coarse = jnp.dot(merged_normed, w_merge, preferred_element_type=jnp.float32).astype(
        jnp.bfloat16
    )
    coarse_normed = layer_norm(coarse.astype(jnp.float32), coarse_gain).astype(jnp.bfloat16)
    gathered = gathered_pieces(coarse_normed, "lat")
    act = jnp.dot(gathered, w_in, preferred_element_type=jnp.float32)
    hidden = activate(act).astype(jnp.bfloat16)
    d_hidden = jnp.einsum("tc,fc->tf", d_gathered, w_out, preferred_element_type=jnp.float32)
    unused, pullback = jax.vjp(activate, act)
    d_act = pullback(d_hidden)[0].astype(jnp.bfloat16)

    def gradient(left, right):
        half = right.shape[1] // 2
        parts = [
            scattered_blocks(
                jnp.einsum(
                    "tc,tf->cf", left, right[:, start : start + half],
                    preferred_element_type=jnp.float32,
                ).astype(jnp.bfloat16),
                "lon",
            )
            for start in (0, half)
        ]
        return jnp.concatenate(parts, axis=1)

    grad_out = gradient(d_gathered, hidden).T
    grad_in = gradient(gathered, d_act)
    mixed = scattered_pieces(jnp.dot(hidden, w_out, preferred_element_type=jnp.float32), "lat")
    coarse_out = (coarse.astype(jnp.float32) + mixed).astype(jnp.bfloat16)
    expanded = jnp.dot(coarse_out, w_expand, preferred_element_type=jnp.float32)
    spread = jnp.concatenate(
        [expanded[:, part * width : (part + 1) * width] for part in range(4)], axis=0
    )
    fields_out = (skip.astype(jnp.float32) + spread).astype(jnp.bfloat16)
    fields_out = picked(order.unmerging, fields_out).reshape(fields_in.shape)
    return (fields_out, grad_in, grad_out)


def solution(mesh):
    placed = (
        P(None, "lat", "lon", None),
        P(None, "lat", "lon"),
        P("lat", "lon"),
        P(),
        P(),
        P(),
        P(),
        P(),
        P(),
        P(),
        P(),
        P(None, "lat"),
        P("lat", None),
        P(),
        P(None, "lat", "lon", None),
    )
    return jax.shard_map(
        on_device,
        mesh=mesh,
        in_specs=placed,
        out_specs=(P(None, "lat", "lon", None), P("lon", "lat"), P("lat", "lon")),
        check_vma=False,
    )
```

```python
import functools
import math

import jax
import jax.numpy as jnp
import numpy as np
from jax import lax
from jax.experimental import pallas as pl
from jax.experimental.pallas import tpu as pltpu
from jax.sharding import PartitionSpec as P


HEADS = 8
WIN_LAT = 12
WIN_LON = 6
SHIFT_LAT = 6
SHIFT_LON = 3


EPSILON = 1e-05


def passed_along(value, axis, steps):
    count = lax.axis_size(axis)
    pairs = [(source, (source + steps) % count) for source in range(count)]
    return lax.ppermute(value, axis, pairs)


def layer_norm(values, gain):
    center = values - jnp.mean(values, axis=-1, keepdims=True)
    spread = jnp.mean(center * center, axis=-1, keepdims=True)
    return center * lax.rsqrt(spread + EPSILON) * gain.astype(jnp.float32)


def activate(values):
    return jax.nn.gelu(values, approximate=True)


def corner_pairs(steps):
    lats, lons = lax.axis_size("lat"), lax.axis_size("lon")
    return [
        (b * lats + a, (b + steps) % lons * lats + (a + steps) % lats)
        for a in range(lats)
        for b in range(lons)
    ]


def swapped(value, axis, bit):
    return lax.ppermute(value, axis, [(place, place ^ bit) for place in range(lax.axis_size(axis))])


def gathered_pieces(block):
    mine, theirs = [block], [swapped(block, "lon", 1)]
    bit = lax.axis_size("lat") // 2
    while bit:
        mine = mine + [swapped(piece, "lat", bit) for piece in mine]
        theirs = theirs + [swapped(piece, "lat", bit) for piece in theirs]
        bit //= 2
    return jnp.concatenate(mine, axis=0), jnp.concatenate(theirs, axis=0)


def own_parity(tokens):
    count = lax.axis_size("lon")
    width = tokens.shape[1] // count
    odd = lax.axis_index("lon") % 2 == 1
    return jnp.concatenate(
        [
            jnp.where(
                odd,
                tokens[:, (start + 1) * width : (start + 2) * width],
                tokens[:, start * width : (start + 1) * width],
            )
            for start in range(0, count, 2)
        ],
        axis=1,
    )


def scattered_pieces(total, axis):
    bit = 1
    while bit < lax.axis_size(axis):
        half = total.shape[0] // 2
        got = swapped(total[half:].astype(jnp.bfloat16), axis, bit)
        total = total[:half] + got.astype(jnp.float32)
        bit *= 2
    return total


def scattered_blocks(totals):
    count = lax.axis_size("lon")
    place = lax.axis_index("lon")
    totals = [
        total.reshape((count // 2, 2 * total.shape[0] // count) + total.shape[1:])
        for total in totals
    ]
    bit = 2
    while bit < count:
        mine = place // bit % 2
        sends, keeps, gots = [], [], []
        for total in totals:
            pairs = total.reshape((total.shape[0] // 2, 2) + total.shape[1:])
            sends.append(lax.dynamic_index_in_dim(pairs, 1 - mine, 1, keepdims=False))
            keeps.append(lax.dynamic_index_in_dim(pairs, mine, 1, keepdims=False))
        for step, send in enumerate(sends):
            if bit == 2 and step >= 2:
                send, gots[step - 2] = lax.optimization_barrier((send, gots[step - 2]))
            gots.append(swapped(send, "lon", bit))
        totals = [
            keep.astype(jnp.float32) + got.astype(jnp.float32) for keep, got in zip(keeps, gots)
        ]
        bit *= 2
        if bit < count:
            totals = [total.astype(jnp.bfloat16) for total in totals]
    return [total[0].astype(jnp.float32) for total in totals]


class TokenOrder:
    def __init__(self, levels, rows, cols):
        self.levels, self.rows, self.cols = levels, rows, cols
        grid = np.arange(levels * rows * cols).reshape(levels, rows, cols)
        blocks = grid.reshape(levels, rows // 2, 2, cols // 2, 2)
        self.merging = blocks.transpose(4, 2, 0, 1, 3).reshape(-1)
        self.unmerging = np.argsort(self.merging)
        place = self.unmerging.reshape(levels, rows, cols)
        windows = grid.reshape(
            levels, rows // WIN_LAT, WIN_LAT, cols // WIN_LON, WIN_LON
        ).transpose(1, 3, 0, 2, 4)
        self.windows = windows.reshape(-1)
        held = np.argsort(self.windows).reshape(levels, rows, cols)
        near, far = slice(None, SHIFT_LAT), slice(SHIFT_LAT, None)
        left, right = slice(None, SHIFT_LON), slice(SHIFT_LON, None)
        self.out_picks, base = self.picks(place, near, far, left, right)
        rolled = np.block([[[place[:, far, right], base[1]], [base[0], base[2]]]])
        self.to_windows = rolled.reshape(-1)[self.windows]
        top, last = slice(None, rows - SHIFT_LAT), slice(rows - SHIFT_LAT, None)
        west, east = slice(None, cols - SHIFT_LON), slice(cols - SHIFT_LON, None)
        self.back_picks, base = self.picks(held, last, top, east, west)
        unrolled = np.block([[[base[2], base[0]], [base[1], held[:, top, west]]]])
        self.to_merging = unrolled.reshape(-1)[self.merging]

    def picks(self, place, edge_rows, inner_rows, edge_cols, inner_cols):
        parts = (
            place[:, edge_rows, inner_cols],
            place[:, inner_rows, edge_cols],
            place[:, edge_rows, edge_cols],
        )
        start, chosen, base = place.size, [], []
        for part in parts:
            padded = -(-part.size // 16) * 16
            chosen.append(np.concatenate([part.reshape(-1), np.full(padded - part.size, -1)]))
            base.append(start + np.arange(part.size).reshape(part.shape))
            start += padded
        return chosen, base


def picked(places, tokens):
    where = jnp.asarray(places, dtype=jnp.int32)
    chosen = where[:, None] == jnp.arange(tokens.shape[0], dtype=jnp.int32)[None, :]
    return jnp.dot(chosen.astype(jnp.bfloat16), tokens, preferred_element_type=jnp.float32).astype(
        jnp.bfloat16
    )


def with_halo(tokens, picks, offset):
    sizes = [len(pick) for pick in picks]
    edges = picked(np.concatenate(picks), tokens)
    row, col = edges[: sizes[0]], edges[sizes[0] : sizes[0] + sizes[1]]
    corner = edges[sizes[0] + sizes[1] :]
    got_row = passed_along(row, "lat", offset)
    got_col = passed_along(col, "lon", offset)
    got_corner = lax.ppermute(corner, ("lon", "lat"), corner_pairs(offset))
    return jnp.concatenate([tokens, got_row, got_col, got_corner], axis=0)


def attention_kernel(width, tokens_ref, weight_ref, mask_ref, out_ref):
    head_size = width // HEADS
    lanes = 2 * head_size
    packed = jnp.dot(tokens_ref[...], weight_ref[...], preferred_element_type=jnp.float32)
    queries = (packed[:, :width] * (1.0 / math.sqrt(head_size))).astype(jnp.bfloat16)
    keys = packed[:, width : 2 * width].astype(jnp.bfloat16)
    values = packed[:, 2 * width :].astype(jnp.bfloat16)
    mask = mask_ref[...]
    first = lax.broadcasted_iota(jnp.int32, (tokens_ref.shape[0], lanes), 1) < head_size
    for pair in range(HEADS // 2):
        span = slice(pair * lanes, (pair + 1) * lanes)
        both, key, value = queries[:, span], keys[:, span], values[:, span]
        results = []
        for query in (jnp.where(first, both, 0), jnp.where(first, 0, both)):
            scores = lax.dot_general(
                query.astype(jnp.bfloat16), key, (((1,), (1,)), ((), ())),
                preferred_element_type=jnp.float32,
            )
            scores = scores + mask
            expos = jnp.exp(scores - jnp.max(scores, axis=-1, keepdims=True))
            total = jnp.sum(expos, axis=-1, keepdims=True)
            mixed = jnp.dot(expos.astype(jnp.bfloat16), value, preferred_element_type=jnp.float32)
            results.append(mixed * (1.0 / total))
        out_ref[:, span] = jnp.where(first, results[0], results[1]).astype(jnp.bfloat16)


def window_attention(tokens, w_qkv, levels, rows, cols, lat_index, lat_total):
    width = tokens.shape[1]
    window = levels * WIN_LAT * WIN_LON
    count_rows, count_cols = rows // WIN_LAT, cols // WIN_LON
    token_row = jnp.arange(window, dtype=jnp.int32) // WIN_LON % WIN_LAT
    block_row = jnp.arange(count_rows, dtype=jnp.int32)
    global_row = lat_index * rows + block_row[:, None] * WIN_LAT + token_row[None, :]
    region = (global_row >= lat_total - WIN_LAT).astype(jnp.int32) + (
        global_row >= lat_total - SHIFT_LAT
    ).astype(jnp.int32)
    mask = jnp.where(region[:, :, None] == region[:, None, :], 0.0, -1e30).astype(jnp.float32)
    return pl.pallas_call(
        functools.partial(attention_kernel, width),
        out_shape=jax.ShapeDtypeStruct(tokens.shape, jnp.bfloat16),
        grid=(count_rows * count_cols,),
        in_specs=[
            pl.BlockSpec((window, width), lambda step: (step, 0)),
            pl.BlockSpec(w_qkv.shape, lambda step: (0, 0)),
            pl.BlockSpec((None, window, window), lambda step: (step // count_cols, 0, 0)),
        ],
        out_specs=pl.BlockSpec((window, width), lambda step: (step, 0)),
        cost_estimate=pl.CostEstimate(
            flops=2 * tokens.shape[0] * width * (3 * width + 2 * window),
            bytes_accessed=4 * tokens.size + 2 * w_qkv.size,
            transcendentals=tokens.shape[0] * window * HEADS,
        ),
    )(tokens, w_qkv, mask)


def side_by_side(tokens):
    count = tokens.shape[0] // 4
    return jnp.concatenate([tokens[part * count : (part + 1) * count] for part in range(4)], axis=1)


def on_device(
    fields_in,
    level_map,
    land_sea,
    level_table,
    surface_table,
    norm_gain,
    w_qkv,
    w_proj,
    merge_gain,
    w_merge,
    coarse_gain,
    w_in,
    w_out,
    w_expand,
    cotangent,
):
    levels, rows, cols, width = fields_in.shape
    count = levels * rows * cols
    order = TokenOrder(levels, rows, cols)
    table_rows = level_table.shape[0]
    level_hot = level_map[..., None] == jnp.arange(table_rows, dtype=jnp.int32)
    sea_hot = (land_sea[..., None] == 1) == (jnp.arange(2, dtype=jnp.int32) == 1)
    sea_hot = jnp.broadcast_to(sea_hot[None], (levels, rows, cols, 2))
    hot = jnp.concatenate([level_hot, sea_hot], axis=-1).astype(jnp.bfloat16)
    hot = picked(order.merging, hot.reshape(count, table_rows + 2))
    tables = jnp.concatenate([level_table, surface_table], axis=0)
    bias = jnp.dot(hot, tables, preferred_element_type=jnp.float32)
    fields = picked(order.merging, fields_in.reshape(count, width)).astype(jnp.float32) + bias
    normed = layer_norm(fields, norm_gain).astype(jnp.bfloat16)
    halo = with_halo(normed, order.out_picks, -1)
    cot_tokens = side_by_side(picked(order.merging, cotangent.reshape(count, width)))
    d_coarse = jnp.einsum(
        "tk,ck->tc", cot_tokens, w_expand, preferred_element_type=jnp.float32
    ).astype(jnp.bfloat16)
    halo, d_coarse = lax.optimization_barrier((halo, d_coarse))
    d_gathered = gathered_pieces(d_coarse)
    windows = picked(order.to_windows, halo)
    lat_total = rows * lax.axis_size("lat")
    attended = window_attention(
        windows, w_qkv, levels, rows, cols, lax.axis_index("lat"), lat_total
    )
    attended = picked(order.to_merging, with_halo(attended, order.back_picks, 1))
    projected = jnp.dot(attended, w_proj, preferred_element_type=jnp.float32)
    skip = (fields + projected).astype(jnp.bfloat16)
    merged_normed = layer_norm(side_by_side(skip).astype(jnp.float32), merge_gain).astype(
        jnp.bfloat16
    )
    coarse = jnp.dot(merged_normed, w_merge, preferred_element_type=jnp.float32).astype(
        jnp.bfloat16
    )
    coarse_normed = layer_norm(coarse.astype(jnp.float32), coarse_gain).astype(jnp.bfloat16)
    gathered = gathered_pieces(coarse_normed)
    hidden, d_act = [], []
    for tokens, d_tokens in zip(gathered, d_gathered):
        act = jnp.dot(tokens, w_in, preferred_element_type=jnp.float32)
        d_hidden = jnp.einsum("tc,fc->tf", d_tokens, w_out, preferred_element_type=jnp.float32)
        value, pullback = jax.vjp(activate, act)
        hidden.append(value.astype(jnp.bfloat16))
        d_act.append(pullback(d_hidden)[0].astype(jnp.bfloat16))
    half = w_in.shape[1] // 2
    totals = []
    for lefts, rights in ((d_gathered, hidden), (gathered, d_act)):
        lefts = [own_parity(left) for left in lefts]
        for start in (0, half):
            total = sum(
                jnp.einsum(
                    "tc,tf->cf", left, right[:, start : start + half],
                    preferred_element_type=jnp.float32,
                )
                for left, right in zip(lefts, rights)
            )
            totals.append(total.astype(jnp.bfloat16))
    sums = scattered_blocks(totals)
    grad_out = jnp.concatenate(sums[:2], axis=1).T
    grad_in = jnp.concatenate(sums[2:], axis=1)
    mixed = scattered_pieces(jnp.dot(hidden[0], w_out, preferred_element_type=jnp.float32), "lat")
    coarse_out = (coarse.astype(jnp.float32) + mixed).astype(jnp.bfloat16)
    expanded = jnp.dot(coarse_out, w_expand, preferred_element_type=jnp.float32)
    spread = jnp.concatenate(
        [expanded[:, part * width : (part + 1) * width] for part in range(4)], axis=0
    )
    fields_out = (skip.astype(jnp.float32) + spread).astype(jnp.bfloat16)
    fields_out = picked(order.unmerging, fields_out).reshape(fields_in.shape)
    return (fields_out, grad_in, grad_out)


def solution(mesh):
    placed = (
        P(None, "lat", "lon", None),
        P(None, "lat", "lon"),
        P("lat", "lon"),
        P(),
        P(),
        P(),
        P(),
        P(),
        P(),
        P(),
        P(),
        P(None, "lat"),
        P("lat", None),
        P(),
        P(None, "lat", "lon", None),
    )
    return jax.shard_map(
        on_device,
        mesh=mesh,
        in_specs=placed,
        out_specs=(P(None, "lat", "lon", None), P("lon", "lat"), P("lat", "lon")),
        check_vma=False,
    )
```

```python
import functools
import math

import jax
import jax.numpy as jnp
import numpy as np
from jax import lax
from jax.experimental import pallas as pl
from jax.experimental.pallas import tpu as pltpu
from jax.sharding import PartitionSpec as P


HEADS = 8
WIN_LAT = 12
WIN_LON = 6
SHIFT_LAT = 6
SHIFT_LON = 3


EPSILON = 1e-05


def passed_along(value, axis, steps):
    count = lax.axis_size(axis)
    pairs = [(source, (source + steps) % count) for source in range(count)]
    return lax.ppermute(value, axis, pairs)


def layer_norm(values, gain):
    center = values - jnp.mean(values, axis=-1, keepdims=True)
    spread = jnp.mean(center * center, axis=-1, keepdims=True)
    return center * lax.rsqrt(spread + EPSILON) * gain.astype(jnp.float32)


def activate(values):
    return jax.nn.gelu(values, approximate=True)


def corner_pairs(steps):
    lats, lons = lax.axis_size("lat"), lax.axis_size("lon")
    return [
        (b * lats + a, (b + steps) % lons * lats + (a + steps) % lats)
        for a in range(lats)
        for b in range(lons)
    ]


def swapped(value, axis, bit):
    return lax.ppermute(value, axis, [(place, place ^ bit) for place in range(lax.axis_size(axis))])


def grown(pieces, bits):
    for bit in bits:
        pieces = pieces + [swapped(piece, "lat", bit) for piece in pieces]
    return pieces


def lat_bits():
    bits, bit = [], lax.axis_size("lat") // 2
    while bit:
        bits.append(bit)
        bit //= 2
    return bits


def by_distance(blocks, bit):
    if len(blocks) == 1:
        return blocks
    flag = lax.axis_index("lon") // bit % 2 == 1
    pairs = list(zip(blocks[0::2], blocks[1::2]))
    near = [jnp.where(flag, high, low) for low, high in pairs]
    far = [jnp.where(flag, low, high) for low, high in pairs]
    return by_distance(near, 2 * bit) + by_distance(far, 2 * bit)


def own_rows(tokens):
    count = lax.axis_size("lon")
    width = tokens.shape[1] // count
    blocks = [tokens[:, start * width : (start + 1) * width] for start in range(count)]
    ordered = by_distance(blocks, 1)
    return jnp.concatenate(ordered[: count // 2], axis=1)


def scattered_pieces(total, axis):
    bit = 1
    while bit < lax.axis_size(axis):
        half = total.shape[0] // 2
        got = swapped(total[half:].astype(jnp.bfloat16), axis, bit)
        total = total[:half] + got.astype(jnp.float32)
        bit *= 2
    return total


def scattered_blocks(makers):
    count = lax.axis_size("lon")
    totals, gots = [], []
    for step, maker in enumerate(makers):
        total = maker(totals)
        half = total.shape[0] // 2
        if count > 2:
            send = total[half:]
            if step >= 2:
                send, gots[step - 2] = lax.optimization_barrier((send, gots[step - 2]))
            gots.append(swapped(send, "lon", 2))
        totals.append(total)
    if count == 2:
        return [total.astype(jnp.float32) for total in totals]
    totals = [
        total[: total.shape[0] // 2].astype(jnp.float32) + got.astype(jnp.float32)
        for total, got in zip(totals, gots)
    ]
    bit = 4
    while bit < count:
        half = totals[0].shape[0] // 2
        gots = [swapped(total[half:].astype(jnp.bfloat16), "lon", bit) for total in totals]
        totals = [total[:half] + got.astype(jnp.float32) for total, got in zip(totals, gots)]
        bit *= 2
    return totals


class TokenOrder:
    def __init__(self, levels, rows, cols):
        self.levels, self.rows, self.cols = levels, rows, cols
        grid = np.arange(levels * rows * cols).reshape(levels, rows, cols)
        blocks = grid.reshape(levels, rows // 2, 2, cols // 2, 2)
        self.merging = blocks.transpose(4, 2, 0, 1, 3).reshape(-1)
        self.unmerging = np.argsort(self.merging)
        place = self.unmerging.reshape(levels, rows, cols)
        windows = grid.reshape(
            levels, rows // WIN_LAT, WIN_LAT, cols // WIN_LON, WIN_LON
        ).transpose(1, 3, 0, 2, 4)
        self.windows = windows.reshape(-1)
        held = np.argsort(self.windows).reshape(levels, rows, cols)
        near, far = slice(None, SHIFT_LAT), slice(SHIFT_LAT, None)
        left, right = slice(None, SHIFT_LON), slice(SHIFT_LON, None)
        self.out_picks, base = self.picks(place, near, far, left, right)
        rolled = np.block([[[place[:, far, right], base[1]], [base[0], base[2]]]])
        self.to_windows = rolled.reshape(-1)[self.windows]
        top, last = slice(None, rows - SHIFT_LAT), slice(rows - SHIFT_LAT, None)
        west, east = slice(None, cols - SHIFT_LON), slice(cols - SHIFT_LON, None)
        self.back_picks, base = self.picks(held, last, top, east, west)
        unrolled = np.block([[[base[2], base[0]], [base[1], held[:, top, west]]]])
        self.to_merging = unrolled.reshape(-1)[self.merging]

    def picks(self, place, edge_rows, inner_rows, edge_cols, inner_cols):
        parts = (
            place[:, edge_rows, inner_cols],
            place[:, inner_rows, edge_cols],
            place[:, edge_rows, edge_cols],
        )
        start, chosen, base = place.size, [], []
        for part in parts:
            padded = -(-part.size // 16) * 16
            chosen.append(np.concatenate([part.reshape(-1), np.full(padded - part.size, -1)]))
            base.append(start + np.arange(part.size).reshape(part.shape))
            start += padded
        return chosen, base


def picked(places, tokens):
    where = jnp.asarray(places, dtype=jnp.int32)
    chosen = where[:, None] == jnp.arange(tokens.shape[0], dtype=jnp.int32)[None, :]
    return jnp.dot(chosen.astype(jnp.bfloat16), tokens, preferred_element_type=jnp.float32).astype(
        jnp.bfloat16
    )


def with_halo(tokens, picks, offset):
    sizes = [len(pick) for pick in picks]
    edges = picked(np.concatenate(picks), tokens)
    row, col = edges[: sizes[0]], edges[sizes[0] : sizes[0] + sizes[1]]
    corner = edges[sizes[0] + sizes[1] :]
    got_row = passed_along(row, "lat", offset)
    got_col = passed_along(col, "lon", offset)
    got_corner = lax.ppermute(corner, ("lon", "lat"), corner_pairs(offset))
    return jnp.concatenate([tokens, got_row, got_col, got_corner], axis=0)


def attention_kernel(width, tokens_ref, weight_ref, mask_ref, out_ref):
    head_size = width // HEADS
    lanes = 2 * head_size
    packed = jnp.dot(tokens_ref[...], weight_ref[...], preferred_element_type=jnp.float32)
    queries = (packed[:, :width] * (1.0 / math.sqrt(head_size))).astype(jnp.bfloat16)
    keys = packed[:, width : 2 * width].astype(jnp.bfloat16)
    values = packed[:, 2 * width :].astype(jnp.bfloat16)
    mask = mask_ref[...]
    first = lax.broadcasted_iota(jnp.int32, (tokens_ref.shape[0], lanes), 1) < head_size
    for pair in range(HEADS // 2):
        span = slice(pair * lanes, (pair + 1) * lanes)
        both, key, value = queries[:, span], keys[:, span], values[:, span]
        results = []
        for query in (jnp.where(first, both, 0), jnp.where(first, 0, both)):
            scores = lax.dot_general(
                query.astype(jnp.bfloat16), key, (((1,), (1,)), ((), ())),
                preferred_element_type=jnp.float32,
            )
            scores = scores + mask
            expos = jnp.exp(scores - jnp.max(scores, axis=-1, keepdims=True))
            total = jnp.sum(expos, axis=-1, keepdims=True)
            mixed = jnp.dot(expos.astype(jnp.bfloat16), value, preferred_element_type=jnp.float32)
            results.append(mixed * (1.0 / total))
        out_ref[:, span] = jnp.where(first, results[0], results[1]).astype(jnp.bfloat16)


def window_attention(tokens, w_qkv, levels, rows, cols, lat_index, lat_total):
    width = tokens.shape[1]
    window = levels * WIN_LAT * WIN_LON
    count_rows, count_cols = rows // WIN_LAT, cols // WIN_LON
    token_row = jnp.arange(window, dtype=jnp.int32) // WIN_LON % WIN_LAT
    block_row = jnp.arange(count_rows, dtype=jnp.int32)
    global_row = lat_index * rows + block_row[:, None] * WIN_LAT + token_row[None, :]
    region = (global_row >= lat_total - WIN_LAT).astype(jnp.int32) + (
        global_row >= lat_total - SHIFT_LAT
    ).astype(jnp.int32)
    mask = jnp.where(region[:, :, None] == region[:, None, :], 0.0, -1e30).astype(jnp.float32)
    return pl.pallas_call(
        functools.partial(attention_kernel, width),
        out_shape=jax.ShapeDtypeStruct(tokens.shape, jnp.bfloat16),
        grid=(count_rows * count_cols,),
        in_specs=[
            pl.BlockSpec((window, width), lambda step: (step, 0)),
            pl.BlockSpec(w_qkv.shape, lambda step: (0, 0)),
            pl.BlockSpec((None, window, window), lambda step: (step // count_cols, 0, 0)),
        ],
        out_specs=pl.BlockSpec((window, width), lambda step: (step, 0)),
        cost_estimate=pl.CostEstimate(
            flops=2 * tokens.shape[0] * width * (3 * width + 2 * window),
            bytes_accessed=4 * tokens.size + 2 * w_qkv.size,
            transcendentals=tokens.shape[0] * window * HEADS,
        ),
    )(tokens, w_qkv, mask)


def side_by_side(tokens):
    count = tokens.shape[0] // 4
    return jnp.concatenate([tokens[part * count : (part + 1) * count] for part in range(4)], axis=1)


def on_device(
    fields_in,
    level_map,
    land_sea,
    level_table,
    surface_table,
    norm_gain,
    w_qkv,
    w_proj,
    merge_gain,
    w_merge,
    coarse_gain,
    w_in,
    w_out,
    w_expand,
    cotangent,
):
    levels, rows, cols, width = fields_in.shape
    count = levels * rows * cols
    order = TokenOrder(levels, rows, cols)
    table_rows = level_table.shape[0]
    level_hot = level_map[..., None] == jnp.arange(table_rows, dtype=jnp.int32)
    sea_hot = (land_sea[..., None] == 1) == (jnp.arange(2, dtype=jnp.int32) == 1)
    sea_hot = jnp.broadcast_to(sea_hot[None], (levels, rows, cols, 2))
    hot = jnp.concatenate([level_hot, sea_hot], axis=-1).astype(jnp.bfloat16)
    hot = picked(order.merging, hot.reshape(count, table_rows + 2))
    tables = jnp.concatenate([level_table, surface_table], axis=0)
    bias = jnp.dot(hot, tables, preferred_element_type=jnp.float32)
    fields = picked(order.merging, fields_in.reshape(count, width)).astype(jnp.float32) + bias
    normed = layer_norm(fields, norm_gain).astype(jnp.bfloat16)
    halo = with_halo(normed, order.out_picks, -1)
    cot_tokens = side_by_side(picked(order.merging, cotangent.reshape(count, width)))
    d_coarse = jnp.einsum(
        "tk,ck->tc", cot_tokens, w_expand, preferred_element_type=jnp.float32
    ).astype(jnp.bfloat16)
    halo, d_coarse = lax.optimization_barrier((halo, d_coarse))
    bits = lat_bits()
    d_mine = grown([d_coarse], bits[:1])
    d_theirs = [swapped(d_coarse, "lon", 1)]
    windows = picked(order.to_windows, halo)
    lat_total = rows * lax.axis_size("lat")
    attended = window_attention(
        windows, w_qkv, levels, rows, cols, lax.axis_index("lat"), lat_total
    )
    attended, d_mine, d_theirs = lax.optimization_barrier((attended, d_mine, d_theirs))
    halo = with_halo(attended, order.back_picks, 1)
    d_theirs = grown(d_theirs, bits[:1])
    d_mine = grown(d_mine, bits[1:])
    halo, d_theirs = lax.optimization_barrier((halo, d_theirs))
    d_theirs = grown(d_theirs, bits[1:])
    d_gathered = jnp.concatenate(d_mine, axis=0), jnp.concatenate(d_theirs, axis=0)
    attended = picked(order.to_merging, halo)
    projected = jnp.dot(attended, w_proj, preferred_element_type=jnp.float32)
    skip = (fields + projected).astype(jnp.bfloat16)
    merged_normed = layer_norm(side_by_side(skip).astype(jnp.float32), merge_gain).astype(
        jnp.bfloat16
    )
    coarse = jnp.dot(merged_normed, w_merge, preferred_element_type=jnp.float32).astype(
        jnp.bfloat16
    )
    coarse_normed = layer_norm(coarse.astype(jnp.float32), coarse_gain).astype(jnp.bfloat16)
    theirs = [swapped(coarse_normed, "lon", 1)]
    mine = grown([coarse_normed], bits)
    theirs = grown(theirs, bits)
    gathered = jnp.concatenate(mine, axis=0), jnp.concatenate(theirs, axis=0)
    hidden, d_act = [], []
    for tokens, d_tokens in zip(gathered, d_gathered):
        act = jnp.dot(tokens, w_in, preferred_element_type=jnp.float32)
        d_hidden = jnp.einsum("tc,fc->tf", d_tokens, w_out, preferred_element_type=jnp.float32)
        value, pullback = jax.vjp(activate, act)
        hidden.append(value.astype(jnp.bfloat16))
        d_act.append(pullback(d_hidden)[0].astype(jnp.bfloat16))
    half = w_in.shape[1] // 2

    def maker(lefts, rights, start):
        def make(before):
            far = rights[1]
            if before:
                far, before[-1] = lax.optimization_barrier((far, before[-1]))
            total = sum(
                jnp.einsum(
                    "tc,tf->cf", left, right[:, start : start + half],
                    preferred_element_type=jnp.float32,
                )
                for left, right in zip(lefts, (rights[0], far))
            )
            return total.astype(jnp.bfloat16)

        return make

    makers = []
    for lefts, rights in ((d_gathered, hidden), (gathered, d_act)):
        lefts = [own_rows(left) for left in lefts]
        makers += [maker(lefts, rights, start) for start in (0, half)]
    sums = scattered_blocks(makers)
    grad_out = jnp.concatenate(sums[:2], axis=1).T
    grad_in = jnp.concatenate(sums[2:], axis=1)
    mixed = scattered_pieces(jnp.dot(hidden[0], w_out, preferred_element_type=jnp.float32), "lat")
    coarse_out = (coarse.astype(jnp.float32) + mixed).astype(jnp.bfloat16)
    expanded = jnp.dot(coarse_out, w_expand, preferred_element_type=jnp.float32)
    spread = jnp.concatenate(
        [expanded[:, part * width : (part + 1) * width] for part in range(4)], axis=0
    )
    fields_out = (skip.astype(jnp.float32) + spread).astype(jnp.bfloat16)
    fields_out = picked(order.unmerging, fields_out).reshape(fields_in.shape)
    return (fields_out, grad_in, grad_out)


def solution(mesh):
    placed = (
        P(None, "lat", "lon", None),
        P(None, "lat", "lon"),
        P("lat", "lon"),
        P(),
        P(),
        P(),
        P(),
        P(),
        P(),
        P(),
        P(),
        P(None, "lat"),
        P("lat", None),
        P(),
        P(None, "lat", "lon", None),
    )
    return jax.shard_map(
        on_device,
        mesh=mesh,
        in_specs=placed,
        out_specs=(P(None, "lat", "lon", None), P("lon", "lat"), P("lat", "lon")),
        check_vma=False,
    )
```

```python
import functools
import math

import jax
import jax.numpy as jnp
import numpy as np
from jax import lax
from jax.experimental import pallas as pl
from jax.experimental.pallas import tpu as pltpu
from jax.sharding import PartitionSpec as P


HEADS = 8
WIN_LAT = 12
WIN_LON = 6
SHIFT_LAT = 6
SHIFT_LON = 3


EPSILON = 1e-05


def passed_along(value, axis, steps):
    count = lax.axis_size(axis)
    pairs = [(source, (source + steps) % count) for source in range(count)]
    return lax.ppermute(value, axis, pairs)


def layer_norm(values, gain):
    center = values - jnp.mean(values, axis=-1, keepdims=True)
    spread = jnp.mean(center * center, axis=-1, keepdims=True)
    return center * lax.rsqrt(spread + EPSILON) * gain.astype(jnp.float32)


def activate(values):
    return jax.nn.gelu(values, approximate=True)


def corner_pairs(steps):
    lats, lons = lax.axis_size("lat"), lax.axis_size("lon")
    return [
        (b * lats + a, (b + steps) % lons * lats + (a + steps) % lats)
        for a in range(lats)
        for b in range(lons)
    ]


def swapped(value, axis, bit):
    return lax.ppermute(value, axis, [(place, place ^ bit) for place in range(lax.axis_size(axis))])


def grown(pieces, bits):
    for bit in bits:
        pieces = pieces + [swapped(piece, "lat", bit) for piece in pieces]
    return pieces


def lat_bits():
    bits, bit = [], lax.axis_size("lat") // 2
    while bit:
        bits.append(bit)
        bit //= 2
    return bits


def by_distance(blocks, bit):
    if len(blocks) == 1:
        return blocks
    flag = lax.axis_index("lon") // bit % 2 == 1
    pairs = list(zip(blocks[0::2], blocks[1::2]))
    near = [jnp.where(flag, high, low) for low, high in pairs]
    far = [jnp.where(flag, low, high) for low, high in pairs]
    return by_distance(near, 2 * bit) + by_distance(far, 2 * bit)


def own_rows(tokens):
    count = lax.axis_size("lon")
    width = tokens.shape[1] // count
    blocks = [tokens[:, start * width : (start + 1) * width] for start in range(count)]
    ordered = by_distance(blocks, 1)
    return jnp.concatenate(ordered[: count // 2], axis=1)


def scattered_pieces(total, axis):
    bit = 1
    while bit < lax.axis_size(axis):
        half = total.shape[0] // 2
        got = swapped(total[half:].astype(jnp.bfloat16), axis, bit)
        total = total[:half] + got.astype(jnp.float32)
        bit *= 2
    return total


def scattered_blocks(makers):
    count = lax.axis_size("lon")
    totals, gots = [], []
    for step, maker in enumerate(makers):
        total = maker(totals)
        half = total.shape[0] // 2
        if count > 2:
            send = total[half:]
            if step >= 3:
                send, gots[step - 2] = lax.optimization_barrier((send, gots[step - 2]))
            gots.append(swapped(send, "lon", 2))
        totals.append(total)
    if count == 2:
        return [total.astype(jnp.float32) for total in totals]
    totals = [
        total[: total.shape[0] // 2].astype(jnp.float32) + got.astype(jnp.float32)
        for total, got in zip(totals, gots)
    ]
    bit = 4
    while bit < count:
        half = totals[0].shape[0] // 2
        gots = [swapped(total[half:].astype(jnp.bfloat16), "lon", bit) for total in totals]
        totals = [total[:half] + got.astype(jnp.float32) for total, got in zip(totals, gots)]
        bit *= 2
    return totals


class TokenOrder:
    def __init__(self, levels, rows, cols):
        self.levels, self.rows, self.cols = levels, rows, cols
        grid = np.arange(levels * rows * cols).reshape(levels, rows, cols)
        blocks = grid.reshape(levels, rows // 2, 2, cols // 2, 2)
        self.merging = blocks.transpose(4, 2, 0, 1, 3).reshape(-1)
        self.unmerging = np.argsort(self.merging)
        place = self.unmerging.reshape(levels, rows, cols)
        windows = grid.reshape(
            levels, rows // WIN_LAT, WIN_LAT, cols // WIN_LON, WIN_LON
        ).transpose(1, 3, 0, 2, 4)
        self.windows = windows.reshape(-1)
        held = np.argsort(self.windows).reshape(levels, rows, cols)
        near, far = slice(None, SHIFT_LAT), slice(SHIFT_LAT, None)
        left, right = slice(None, SHIFT_LON), slice(SHIFT_LON, None)
        self.out_picks, base = self.picks(place, near, far, left, right)
        rolled = np.block([[[place[:, far, right], base[1]], [base[0], base[2]]]])
        self.to_windows = rolled.reshape(-1)[self.windows]
        top, last = slice(None, rows - SHIFT_LAT), slice(rows - SHIFT_LAT, None)
        west, east = slice(None, cols - SHIFT_LON), slice(cols - SHIFT_LON, None)
        self.back_picks, base = self.picks(held, last, top, east, west)
        unrolled = np.block([[[base[2], base[0]], [base[1], held[:, top, west]]]])
        self.to_merging = unrolled.reshape(-1)[self.merging]

    def picks(self, place, edge_rows, inner_rows, edge_cols, inner_cols):
        parts = (
            place[:, edge_rows, inner_cols],
            place[:, inner_rows, edge_cols],
            place[:, edge_rows, edge_cols],
        )
        start, chosen, base = place.size, [], []
        for part in parts:
            padded = -(-part.size // 16) * 16
            chosen.append(np.concatenate([part.reshape(-1), np.full(padded - part.size, -1)]))
            base.append(start + np.arange(part.size).reshape(part.shape))
            start += padded
        return chosen, base


def picked(places, tokens):
    where = jnp.asarray(places, dtype=jnp.int32)
    chosen = where[:, None] == jnp.arange(tokens.shape[0], dtype=jnp.int32)[None, :]
    return jnp.dot(chosen.astype(jnp.bfloat16), tokens, preferred_element_type=jnp.float32).astype(
        jnp.bfloat16
    )


def with_halo(tokens, picks, offset):
    sizes = [len(pick) for pick in picks]
    edges = picked(np.concatenate(picks), tokens)
    row, col = edges[: sizes[0]], edges[sizes[0] : sizes[0] + sizes[1]]
    corner = edges[sizes[0] + sizes[1] :]
    got_row = passed_along(row, "lat", offset)
    got_col = passed_along(col, "lon", offset)
    got_corner = lax.ppermute(corner, ("lon", "lat"), corner_pairs(offset))
    return jnp.concatenate([tokens, got_row, got_col, got_corner], axis=0)


def attention_kernel(width, tokens_ref, weight_ref, mask_ref, out_ref):
    head_size = width // HEADS
    lanes = 2 * head_size
    packed = jnp.dot(tokens_ref[...], weight_ref[...], preferred_element_type=jnp.float32)
    queries = (packed[:, :width] * (1.0 / math.sqrt(head_size))).astype(jnp.bfloat16)
    keys = packed[:, width : 2 * width].astype(jnp.bfloat16)
    values = packed[:, 2 * width :].astype(jnp.bfloat16)
    mask = mask_ref[...]
    first = lax.broadcasted_iota(jnp.int32, (tokens_ref.shape[0], lanes), 1) < head_size
    for pair in range(HEADS // 2):
        span = slice(pair * lanes, (pair + 1) * lanes)
        both, key, value = queries[:, span], keys[:, span], values[:, span]
        results = []
        for query in (jnp.where(first, both, 0), jnp.where(first, 0, both)):
            scores = lax.dot_general(
                query.astype(jnp.bfloat16), key, (((1,), (1,)), ((), ())),
                preferred_element_type=jnp.float32,
            )
            scores = scores + mask
            expos = jnp.exp(scores - jnp.max(scores, axis=-1, keepdims=True))
            total = jnp.sum(expos, axis=-1, keepdims=True)
            mixed = jnp.dot(expos.astype(jnp.bfloat16), value, preferred_element_type=jnp.float32)
            results.append(mixed * (1.0 / total))
        out_ref[:, span] = jnp.where(first, results[0], results[1]).astype(jnp.bfloat16)


def window_attention(tokens, w_qkv, levels, rows, cols, lat_index, lat_total):
    width = tokens.shape[1]
    window = levels * WIN_LAT * WIN_LON
    count_rows, count_cols = rows // WIN_LAT, cols // WIN_LON
    token_row = jnp.arange(window, dtype=jnp.int32) // WIN_LON % WIN_LAT
    block_row = jnp.arange(count_rows, dtype=jnp.int32)
    global_row = lat_index * rows + block_row[:, None] * WIN_LAT + token_row[None, :]
    region = (global_row >= lat_total - WIN_LAT).astype(jnp.int32) + (
        global_row >= lat_total - SHIFT_LAT
    ).astype(jnp.int32)
    mask = jnp.where(region[:, :, None] == region[:, None, :], 0.0, -1e30).astype(jnp.float32)
    return pl.pallas_call(
        functools.partial(attention_kernel, width),
        out_shape=jax.ShapeDtypeStruct(tokens.shape, jnp.bfloat16),
        grid=(count_rows * count_cols,),
        in_specs=[
            pl.BlockSpec((window, width), lambda step: (step, 0)),
            pl.BlockSpec(w_qkv.shape, lambda step: (0, 0)),
            pl.BlockSpec((None, window, window), lambda step: (step // count_cols, 0, 0)),
        ],
        out_specs=pl.BlockSpec((window, width), lambda step: (step, 0)),
        cost_estimate=pl.CostEstimate(
            flops=2 * tokens.shape[0] * width * (3 * width + 2 * window),
            bytes_accessed=4 * tokens.size + 2 * w_qkv.size,
            transcendentals=tokens.shape[0] * window * HEADS,
        ),
    )(tokens, w_qkv, mask)


def side_by_side(tokens):
    count = tokens.shape[0] // 4
    return jnp.concatenate([tokens[part * count : (part + 1) * count] for part in range(4)], axis=1)


def on_device(
    fields_in,
    level_map,
    land_sea,
    level_table,
    surface_table,
    norm_gain,
    w_qkv,
    w_proj,
    merge_gain,
    w_merge,
    coarse_gain,
    w_in,
    w_out,
    w_expand,
    cotangent,
):
    levels, rows, cols, width = fields_in.shape
    count = levels * rows * cols
    order = TokenOrder(levels, rows, cols)
    table_rows = level_table.shape[0]
    level_hot = level_map[..., None] == jnp.arange(table_rows, dtype=jnp.int32)
    sea_hot = (land_sea[..., None] == 1) == (jnp.arange(2, dtype=jnp.int32) == 1)
    sea_hot = jnp.broadcast_to(sea_hot[None], (levels, rows, cols, 2))
    hot = jnp.concatenate([level_hot, sea_hot], axis=-1).astype(jnp.bfloat16)
    hot = picked(order.merging, hot.reshape(count, table_rows + 2))
    tables = jnp.concatenate([level_table, surface_table], axis=0)
    bias = jnp.dot(hot, tables, preferred_element_type=jnp.float32)
    fields = picked(order.merging, fields_in.reshape(count, width)).astype(jnp.float32) + bias
    normed = layer_norm(fields, norm_gain).astype(jnp.bfloat16)
    halo = with_halo(normed, order.out_picks, -1)
    cot_tokens = side_by_side(picked(order.merging, cotangent.reshape(count, width)))
    d_coarse = jnp.einsum(
        "tk,ck->tc", cot_tokens, w_expand, preferred_element_type=jnp.float32
    ).astype(jnp.bfloat16)
    halo, d_coarse = lax.optimization_barrier((halo, d_coarse))
    bits = lat_bits()
    d_mine = grown([d_coarse], bits[:1])
    d_theirs = [swapped(d_coarse, "lon", 1)]
    windows = picked(order.to_windows, halo)
    lat_total = rows * lax.axis_size("lat")
    attended = window_attention(
        windows, w_qkv, levels, rows, cols, lax.axis_index("lat"), lat_total
    )
    attended, d_mine, d_theirs = lax.optimization_barrier((attended, d_mine, d_theirs))
    halo = with_halo(attended, order.back_picks, 1)
    d_theirs = grown(d_theirs, bits[:1])
    d_mine = grown(d_mine, bits[1:])
    halo, d_theirs = lax.optimization_barrier((halo, d_theirs))
    d_theirs = grown(d_theirs, bits[1:])
    attended = picked(order.to_merging, halo)
    projected = jnp.dot(attended, w_proj, preferred_element_type=jnp.float32)
    skip = (fields + projected).astype(jnp.bfloat16)
    merged_normed = layer_norm(side_by_side(skip).astype(jnp.float32), merge_gain).astype(
        jnp.bfloat16
    )
    coarse = jnp.dot(merged_normed, w_merge, preferred_element_type=jnp.float32).astype(
        jnp.bfloat16
    )
    coarse_normed = layer_norm(coarse.astype(jnp.float32), coarse_gain).astype(jnp.bfloat16)
    theirs = [swapped(coarse_normed, "lon", 1)]
    mine = grown([coarse_normed], bits[:1])
    mine, theirs, d_theirs = lax.optimization_barrier((mine, theirs, d_theirs))
    mine = grown(mine, bits[1:])
    theirs = grown(theirs, bits)
    d_gathered = jnp.concatenate(d_mine, axis=0), jnp.concatenate(d_theirs, axis=0)
    gathered = jnp.concatenate(mine, axis=0), jnp.concatenate(theirs, axis=0)
    hidden, d_act = [], []
    for tokens, d_tokens in zip(gathered, d_gathered):
        act = jnp.dot(tokens, w_in, preferred_element_type=jnp.float32)
        d_hidden = jnp.einsum("tc,fc->tf", d_tokens, w_out, preferred_element_type=jnp.float32)
        value, pullback = jax.vjp(activate, act)
        hidden.append(value.astype(jnp.bfloat16))
        d_act.append(pullback(d_hidden)[0].astype(jnp.bfloat16))
    half = w_in.shape[1] // 2

    def maker(lefts, rights, start):
        def make(before):
            far = rights[1]
            if before:
                far, before[-1] = lax.optimization_barrier((far, before[-1]))
            total = sum(
                jnp.einsum(
                    "tc,tf->cf", left, right[:, start : start + half],
                    preferred_element_type=jnp.float32,
                )
                for left, right in zip(lefts, (rights[0], far))
            )
            return total.astype(jnp.bfloat16)

        return make

    makers = []
    for lefts, rights in ((d_gathered, hidden), (gathered, d_act)):
        lefts = [own_rows(left) for left in lefts]
        makers += [maker(lefts, rights, start) for start in (0, half)]
    sums = scattered_blocks(makers)
    grad_out = jnp.concatenate(sums[:2], axis=1).T
    grad_in = jnp.concatenate(sums[2:], axis=1)
    mixed = scattered_pieces(jnp.dot(hidden[0], w_out, preferred_element_type=jnp.float32), "lat")
    coarse_out = (coarse.astype(jnp.float32) + mixed).astype(jnp.bfloat16)
    expanded = jnp.dot(coarse_out, w_expand, preferred_element_type=jnp.float32)
    spread = jnp.concatenate(
        [expanded[:, part * width : (part + 1) * width] for part in range(4)], axis=0
    )
    fields_out = (skip.astype(jnp.float32) + spread).astype(jnp.bfloat16)
    fields_out = picked(order.unmerging, fields_out).reshape(fields_in.shape)
    return (fields_out, grad_in, grad_out)


def solution(mesh):
    placed = (
        P(None, "lat", "lon", None),
        P(None, "lat", "lon"),
        P("lat", "lon"),
        P(),
        P(),
        P(),
        P(),
        P(),
        P(),
        P(),
        P(),
        P(None, "lat"),
        P("lat", None),
        P(),
        P(None, "lat", "lon", None),
    )
    return jax.shard_map(
        on_device,
        mesh=mesh,
        in_specs=placed,
        out_specs=(P(None, "lat", "lon", None), P("lon", "lat"), P("lat", "lon")),
        check_vma=False,
    )
```
